32 devices in a mesh: lvl: 2 (over x), lat: 4 (over z), lon: 4 (over y, core).
Axes of the slice: x: 2, y: 2, z: 4, core: 2. Of those that a mesh axis runs over, the one named last changes fastest.
Arguments:
- patches: bfloat16 [2, 2, 24, 48, 1000], P('lvl', None, 'lat', 'lon'), may hold values from -6 to 6
- level_embed: float32 [2, 512], P('lvl'), may hold values from -6 to 6
- embed_weight: bfloat16 [1000, 512], replicated, may hold values from -0.1875 to 0.1875
- block_ids: int32 [2, 2, 4, 4, 3], P('lvl', None, 'lat', 'lon'), may hold values from -1 to 5, as said below
- latent_queries: bfloat16 [4, 512], replicated, may hold values from -6 to 6
- cross_gain: float32 [512], replicated, may hold values from 0.1 to 1.9
- cross_query: bfloat16 [512, 512], replicated, may hold values from -0.25 to 0.25
- cross_kv: bfloat16 [512, 1024], replicated, may hold values from -0.25 to 0.25
- cross_out: bfloat16 [512, 512], replicated, may hold values from -0.25 to 0.25
- region_ids: int32 [48, 48], P(('lvl', 'lat'), 'lon'), may hold values from 0 to 2
- swin_gain: float32 [512], replicated, may hold values from 0.1 to 1.9
- swin_qkv: bfloat16 [512, 1536], replicated, may hold values from -0.25 to 0.25
- swin_out: bfloat16 [512, 512], replicated, may hold values from -0.25 to 0.25
- mlp_gain: float32 [512], replicated, may hold values from 0.1 to 1.9
- mlp_up: bfloat16 [512, 2048], replicated, may hold values from -0.25 to 0.25
- mlp_down: bfloat16 [2048, 512], replicated, may hold values from -0.125 to 0.125
Outputs:
- latents: float32 [4, 48, 48, 512], P(None, ('lvl', 'lat'), 'lon')
The draws below stay inside these ranges and needn't reach their ends.
Inputs may be any that keep to these rules, and one draw needn't show every extreme that they name: block_ids[l, m, a, o, :] lists the column blocks b (longitude column (m * 4 + a) * 6 + b, latitude rows o * 12 to o * 12 + 11) at which level l is present: distinct numbers in its first slots, -1 in the remaining slots. Every column block is named by the list of at least one level. For every band and tile, the list of some level fills all 3 slots.
All inputs are finite; a program needn't handle non-finite values.
Results may differ from the reference program's by a relative error of at most 0.005.
Values may be sent and summed in bfloat16 or wider, within the bound.
A program may use at most 64 MiB of HBM per device.

```python
import math
import jax
import jax.numpy as jnp
from jax import lax

D = 512
HEADS = 16
MLP = 2048
PF = 1000
LATENT = 4
WIN_LV = 2
WIN_LAT = 6
WIN_LON = 12
SH = 6
SW = 12
LEVELS = 2
BANDS = 2
LAT_TILES = 4
LON_TILES = 4
CAP = 3
NH = 48
NW = 48


def draw_block_ids(key, part):
    key_shuffle = jax.random.fold_in(key, 11)
    key_count = jax.random.fold_in(key, 12)
    key_full = jax.random.fold_in(key, 13)
    key_pick = jax.random.fold_in(key, 14)
    groups = (BANDS, LAT_TILES, LON_TILES)
    block_index = jnp.arange(SH, dtype=jnp.int32)
    shuffle = jax.random.randint(key_shuffle, groups + (SH,), 0, 1 << 20) * SH + block_index
    permuted = jnp.argsort(shuffle, axis=-1)
    position = jnp.argsort(permuted, axis=-1)
    duty_level = position % LEVELS
    level_index = jnp.arange(LEVELS, dtype=jnp.int32)
    required = (duty_level[None] == level_index[:, None, None, None, None]).astype(jnp.int32)
    need_count = jnp.sum(required, axis=-1)
    slot_count = jax.random.randint(key_count, need_count.shape, need_count, CAP + 1)
    full_level = jax.random.randint(key_full, groups, 0, LEVELS)
    slot_count = jnp.where(level_index[:, None, None, None] == full_level[None], CAP, slot_count)
    priority = jax.random.randint(key_pick, required.shape, 0, 1 << 20) * SH + block_index + required * (1 << 27)
    chosen = jnp.argsort(-priority, axis=-1)[..., :CAP].astype(jnp.int32)
    slot_index = jnp.arange(CAP, dtype=jnp.int32)
    return jnp.where(slot_index < slot_count[..., None], chosen, -1).astype(jnp.int32)


def plant(array, key, low, high):
    dims = array.shape
    place = [jax.random.randint(jax.random.fold_in(key, axis), (), 0, dims[axis]) for axis in range(len(dims))]
    array = array.at[tuple(place)].set(low)
    longest = dims.index(max(dims))
    place[longest] = (place[longest] + 1) % dims[longest]
    return array.at[tuple(place)].set(high)


def shard_levels(own_key, dims, cuts, smallest, high):
    loudness, own = 1.0, jax.random.fold_in(own_key, 6)
    for dim, blocks in cuts:
        draws = jnp.exp(jax.random.uniform(jax.random.fold_in(own, dim), (blocks,), jnp.float32, smallest / len(cuts), high / len(cuts)))
        loudness = loudness * jnp.repeat(draws, dims[dim] // blocks).reshape([-1 if axis == dim else 1 for axis in range(len(dims))])
    return loudness


def scatter_about(stream_key, dims, width, reach, split=(), kind=jnp.bfloat16):
    gain = shard_levels(stream_key, dims, split, -0.22, 0.18) if split else 1.0
    values = jax.random.normal(stream_key, dims, jnp.float32) * width * gain
    return jnp.minimum(jnp.maximum(values, -reach), reach).astype(kind)


def setup_inputs(seed: int = 0) -> dict:
    splits = jax.random.split(jax.random.key(seed), 17)
    return {
        "patches": scatter_about(splits[0], (LEVELS, BANDS, LAT_TILES * SH, NW, PF), 1.0, 6.0, ((0, 2), (2, 4), (3, 4))),
        "level_embed": scatter_about(splits[1], (LEVELS, D), 1.0, 6.0, ((0, 2),), jnp.float32),
        "embed_weight": scatter_about(splits[2], (PF, D), PF ** -0.5, 0.1875),
        "block_ids": draw_block_ids(jax.random.fold_in(splits[16], 71), 0),
        "latent_queries": scatter_about(splits[4], (LATENT, D), 1.0, 6.0),
        "cross_gain": jnp.clip(1.0 + 0.18 * jax.random.normal(splits[5], (D,), jnp.float32), 0.1, 1.9),
        "cross_query": scatter_about(splits[6], (D, D), D ** -0.5, 0.25),
        "cross_kv": scatter_about(splits[7], (D, 2 * D), D ** -0.5, 0.25),
        "cross_out": scatter_about(splits[8], (D, D), D ** -0.5, 0.25),
        "region_ids": plant(jax.random.randint(splits[9], (NH, NW), 0, 3), jax.random.fold_in(splits[9], 1), 0, 2).astype(jnp.int32),
        "swin_gain": jnp.clip(1.0 + 0.18 * jax.random.normal(splits[10], (D,), jnp.float32), 0.1, 1.9),
        "swin_qkv": scatter_about(splits[11], (D, 3 * D), D ** -0.5, 0.25),
        "swin_out": scatter_about(splits[12], (D, D), D ** -0.5, 0.25),
        "mlp_gain": jnp.clip(1.0 + 0.18 * jax.random.normal(splits[13], (D,), jnp.float32), 0.1, 1.9),
        "mlp_up": scatter_about(splits[14], (D, MLP), D ** -0.5, 0.25),
        "mlp_down": scatter_about(splits[15], (MLP, D), MLP ** -0.5, 0.125),
    }


def layer_norm(tensor, gain_vec):
    average = lax.optimization_barrier(jnp.mean(tensor, axis=-1, keepdims=True))
    centred = tensor - average
    spread = lax.optimization_barrier(jnp.mean(centred * centred, axis=-1, keepdims=True))
    return centred * lax.rsqrt(spread + 1e-05) * gain_vec

def to_windows(tensor, spans):
    trailing = tensor.shape[3:]
    level_span, row_span, col_span = tensor.shape[:3]
    first, second, third = spans
    shaped = tensor.reshape((level_span // first, first, row_span // second, second, col_span // third, third) + trailing)
    axes_order = (0, 2, 4, 1, 3, 5) + tuple(range(6, 6 + len(trailing)))
    return shaped.transpose(axes_order).reshape((level_span // first, row_span // second, col_span // third, first * second * third) + trailing)

def from_windows(tensor, extents, spans):
    trailing = tensor.shape[4:]
    level_span, row_span, col_span = extents
    first, second, third = spans
    shaped = tensor.reshape((level_span // first, row_span // second, col_span // third, first, second, third) + trailing)
    axes_order = (0, 3, 1, 4, 2, 5) + tuple(range(6, 6 + len(trailing)))
    return shaped.transpose(axes_order).reshape((level_span, row_span, col_span) + trailing)

def label_windows(labels, spans):
    row_span, col_span = labels.shape
    second, third = spans
    shaped = labels.reshape(row_span // second, second, col_span // third, third).transpose(0, 2, 1, 3)
    shaped = shaped.reshape(row_span // second, col_span // third, second * third)
    return jnp.concatenate([shaped] * WIN_LV, axis=-1)

def window_attend(queries, key_rows, value_rows, usable, labels):
    window_size = queries.shape[3]
    scores = jnp.einsum('abcqhe,abckhe->abchqk', queries.astype(jnp.float32), key_rows.astype(jnp.float32))
    same_label = labels[:, :, :, None] == labels[:, :, None, :]
    allowed = usable[:, :, :, None, None, :] & same_label[None, :, :, None, :, :]
    allowed = allowed | jnp.eye(window_size, dtype=jnp.bool_)
    exponent = jnp.where(allowed, jnp.exp(scores), jnp.zeros_like(scores))
    weights = (exponent / lax.optimization_barrier(jnp.sum(exponent, axis=-1, keepdims=True))).astype(jnp.bfloat16)
    mixture = jnp.einsum('abchqk,abckhe->abcqhe', weights.astype(jnp.float32), value_rows.astype(jnp.float32))
    return mixture.astype(jnp.bfloat16)

def reference(patches, level_embed, embed_weight, block_ids, latent_queries, cross_gain, cross_query, cross_kv, cross_out, region_ids, swin_gain, swin_qkv, swin_out, mlp_gain, mlp_up, mlp_down):
    head_dim = D // HEADS
    inv_root = 1.0 / math.sqrt(head_dim)
    band_rows = LAT_TILES * SH
    matches = jnp.any(block_ids[..., None] == jnp.arange(SH, dtype=jnp.int32), axis=4)
    matches = jnp.transpose(matches, (0, 1, 2, 4, 3)).reshape(LEVELS, BANDS, band_rows, LON_TILES)
    presence = jnp.repeat(matches.astype(jnp.float32), SW, axis=3)
    cross_queries = jnp.dot(latent_queries, cross_query, preferred_element_type=jnp.float32) * inv_root
    cross_queries = cross_queries.astype(jnp.bfloat16).reshape(LATENT, HEADS, head_dim)

    def one_band(inputs):
        band_patches, band_presence = inputs
        embedded = jnp.dot(band_patches.reshape(-1, PF), embed_weight, preferred_element_type=jnp.float32)
        embedded = embedded.reshape(LEVELS, band_rows, NW, D) + level_embed[:, None, None, :]
        embedded = embedded.astype(jnp.bfloat16)
        keys_in = layer_norm(embedded.astype(jnp.float32), cross_gain).astype(jnp.bfloat16)
        key_value = jnp.dot(keys_in.reshape(-1, D), cross_kv, preferred_element_type=jnp.float32).astype(jnp.bfloat16)
        key_value = key_value.reshape(LEVELS, band_rows, NW, 2, HEADS, head_dim)
        scores = jnp.einsum('qhe,lrche->qhlrc', cross_queries.astype(jnp.float32), key_value[:, :, :, 0].astype(jnp.float32))
        exponent = jnp.exp(scores) * band_presence[None, None]
        weights = (exponent / lax.optimization_barrier(jnp.sum(exponent, axis=2, keepdims=True))).astype(jnp.bfloat16)
        mixture = jnp.einsum('qhlrc,lrche->qrche', weights.astype(jnp.float32), key_value[:, :, :, 1].astype(jnp.float32))
        mixture = mixture.astype(jnp.bfloat16).reshape(-1, D)
        projected = jnp.dot(mixture, cross_out, preferred_element_type=jnp.float32).reshape(LATENT, band_rows, NW, D)
        return latent_queries.astype(jnp.float32)[:, None, None, :] + projected
    starts = lax.map(one_band, (jnp.moveaxis(patches, 1, 0), jnp.moveaxis(presence, 1, 0)))
    latent_start = jnp.moveaxis(starts, 0, 1).reshape(LATENT, NH, NW, D)
    normed = layer_norm(latent_start, swin_gain).astype(jnp.bfloat16)
    projected = jnp.dot(normed.reshape(-1, D), swin_qkv, preferred_element_type=jnp.float32)
    projected = projected.reshape(LATENT, NH, NW, 3, HEADS, head_dim)
    queries = (projected[:, :, :, 0] * inv_root).astype(jnp.bfloat16)
    key_rows = projected[:, :, :, 1].astype(jnp.bfloat16)
    value_rows = projected[:, :, :, 2].astype(jnp.bfloat16)
    level_pad = WIN_LV // 2
    col_margin = WIN_LAT // 2
    spans = (WIN_LV, WIN_LON, WIN_LAT)
    widths = ((level_pad, level_pad), (0, 0), (col_margin, col_margin), (0, 0), (0, 0))
    usable = jnp.pad(jnp.ones((LATENT, NH, NW), jnp.bool_), widths[:3])
    labels = jnp.pad(region_ids, ((0, 0), (col_margin, col_margin)))
    window_labels = label_windows(labels, (WIN_LON, WIN_LAT))
    inputs = (jnp.moveaxis(to_windows(jnp.pad(queries, widths), spans), 1, 0), jnp.moveaxis(to_windows(jnp.pad(key_rows, widths), spans), 1, 0), jnp.moveaxis(to_windows(jnp.pad(value_rows, widths), spans), 1, 0), jnp.moveaxis(to_windows(usable, spans), 1, 0), window_labels)

    def one_row(pieces):
        q_part, k_part, v_part, u_part, l_part = pieces
        return window_attend(q_part[:, None], k_part[:, None], v_part[:, None], u_part[:, None], l_part[None])[:, 0]
    mixture = jnp.moveaxis(lax.map(one_row, inputs), 0, 1)
    mixture = from_windows(mixture, (LATENT + 2 * level_pad, NH, NW + 2 * col_margin), spans)
    mixture = mixture[level_pad:level_pad + LATENT, :, col_margin:col_margin + NW]
    mixture = mixture.reshape(-1, D)
    attended = latent_start + jnp.dot(mixture, swin_out, preferred_element_type=jnp.float32).reshape(LATENT, NH, NW, D)
    mlp_in = layer_norm(attended, mlp_gain).astype(jnp.bfloat16).reshape(-1, D)
    hidden = jnp.dot(mlp_in, mlp_up, preferred_element_type=jnp.float32)
    activated = jax.nn.gelu(hidden, approximate=False).astype(jnp.bfloat16)
    lowered = jnp.dot(activated, mlp_down, preferred_element_type=jnp.float32).reshape(LATENT, NH, NW, D)
    return attended + lowered
```

```python
import functools
import math

import jax
import jax.numpy as jnp
import numpy as np
from jax import lax
from jax.experimental import pallas as pl
from jax.experimental.pallas import tpu as pltpu
from jax.sharding import PartitionSpec as P

HEADS = 16
WIN_LAT = 6
BLOCK = 16
CODE = 64
MESH = pl.DeviceIdType.MESH
F32 = jnp.float32
BF16 = jnp.bfloat16


def layer_norm(tensor, gain_vec):
    average = jnp.mean(tensor, axis=-1, keepdims=True)
    centred = tensor - average
    spread = jnp.mean(centred * centred, axis=-1, keepdims=True)
    return centred * lax.rsqrt(spread + 1e-05) * gain_vec


def mm(a, b):
    return jnp.dot(a, b, preferred_element_type=F32)


def mm_nt(a, b):
    return lax.dot_general(a, b, (((1,), (1,)), ((), ())), preferred_element_type=F32)


class Plan:
    def __init__(self, rows, cols, cap):
        self.rows, self.cols, self.cap = rows, cols, cap
        self.margin = WIN_LAT // 2
        per = (BLOCK - 1) // cap
        assert per >= self.margin and rows < CODE and rows * cols <= 128
        self.blocks = max(2, -(-cols // per))
        spread = [min(per, cols)]
        middle = cols - 2 * per
        assert middle >= 0
        groups = [list(range(per))]
        groups += [list(range(c, min(c + per, cols - per))) for c in range(per, cols - per, per)]
        groups += [list(range(cols - per, cols))]
        self.blocks = len(groups)
        self.tile_rows = self.blocks * BLOCK
        col_of = np.full((self.blocks, BLOCK), -1)
        for b, group in enumerate(groups):
            for k, c in enumerate(group):
                col_of[b, k * cap : (k + 1) * cap] = c
        self.col_of = col_of.reshape(-1)
        self.tiles = [(0, self.tile_rows), (self.tile_rows, self.tile_rows)]
        self.tiles += [(2 * self.tile_rows + k * BLOCK, BLOCK) for k in range(4)]
        self.wide_rows = 2 * self.tile_rows + 4 * BLOCK
        first, last = self.col_of[:BLOCK], self.col_of[-BLOCK:]
        parts = [self.col_of, self.col_of, last, last, first, first]
        row_code = np.concatenate(
            [np.where(p >= 0, (t * cols + p) * CODE, -100000) for t, p in enumerate(parts)]
        )
        lanes = -(-self.wide_rows // 128) * 128
        self.lanes = lanes
        self.row_code = np.full((8, lanes), -100000, np.int32)
        self.row_code[:, : self.wide_rows] = row_code
        m = self.margin
        spans = [range(cols), range(cols), range(cols - m, cols), range(cols - m, cols), range(m), range(m)]
        offset = [0, 0, -cols, -cols, cols, cols]
        cells = [(t, i, j, (j + offset[t] + m) // WIN_LAT) for t in range(6) for i in range(rows) for j in spans[t]]
        self.cells = np.array(cells)
        self.count = len(cells)
        self.own = rows * cols
        self.info = np.zeros((self.count, 128), np.int32)
        t, i, j, win = self.cells.T
        self.info[:, 0] = (t * cols + j) * CODE + i
        self.info[:, 1] = i * cols + j
        self.info[:, 2] = t
        self.win = (win[: self.own, None] == win[None, :]).astype(np.float32)


def send_kernel(plan, names, sizes, patches, level_embed, weight, ids, labels, out, wbuf, buf, wsem, send, recv, local):
    rows, cols, cap = plan.rows, plan.cols, plan.cap
    levels, lat_count, lon_count = sizes
    width = weight.shape[1]
    load = pltpu.make_async_copy(weight, wbuf, wsem)
    load.start()
    me_l, me_a, me_o = (lax.axis_index(name) for name in names)
    low_bit = lax.rem(me_a, 2)
    partner = me_a + 1 - 2 * low_bit
    lats = (me_a, partner)
    lons = {
        0: me_o,
        1: lax.rem(me_o + 1, lon_count),
        -1: lax.rem(me_o + lon_count - 1, lon_count),
    }
    moves = [
        (dm, da, do)
        for dm in range(levels)
        for da in (0, 1)
        for do in (0, -1, 1)
        if (dm, da, do) != (0, 0, 0)
    ]
    band_of = [lax.rem(me_l + dm, levels) for dm in range(levels)]
    barrier = pltpu.get_barrier_semaphore()
    for dm, da, do in moves:
        pl.semaphore_signal(
            barrier, inc=1, device_id=(band_of[dm], lats[da], lons[do]), device_id_type=MESH
        )

    tile_rows = plan.tile_rows
    row = lax.broadcasted_iota(jnp.int32, (tile_rows, 1), 0)
    col_of = jnp.full((tile_rows, 1), -1, jnp.int32)
    slot_of = jnp.full((tile_rows, 1), -1, jnp.int32)
    for r in range(tile_rows):
        pass
    in_block = jnp.bitwise_and(row, BLOCK - 1)
    base = jnp.zeros((tile_rows, 1), jnp.int32)
    for b in range(plan.blocks):
        start = int(plan.col_of[b * BLOCK])
        base = jnp.where((row >= b * BLOCK) & (row < (b + 1) * BLOCK), start, base)
    col_step = jnp.zeros((tile_rows, 1), jnp.int32)
    for k in range(1, BLOCK // cap + 1):
        col_step = col_step + (in_block >= k * cap).astype(jnp.int32)
    slot_of = in_block - col_step * cap
    col_of = base + col_step
    used = jnp.zeros((tile_rows, 1), jnp.bool_)
    for b in range(plan.blocks):
        n = int((plan.col_of[b * BLOCK : (b + 1) * BLOCK] >= 0).sum())
        used = used | ((row >= b * BLOCK) & (row < b * BLOCK + n))
    cell = lax.broadcasted_iota(jnp.int32, (128, 1), 0)
    cell_i = jnp.zeros((128, 1), jnp.int32)
    for k in range(1, rows):
        cell_i = cell_i + (cell >= k * cols).astype(jnp.int32)
    cell_j = cell - cell_i * cols
    lab = labels[...].astype(F32)
    col_lab = jnp.zeros((128, cols), F32)
    for k in range(rows):
        col_lab = jnp.where(cell_i == k, lab[k : k + 1, :], col_lab)
    picked_j = lax.broadcasted_iota(jnp.int32, (128, cols), 1) == cell_j
    lab_col = jnp.sum(jnp.where(picked_j, col_lab, 0.0), axis=1, keepdims=True)
    eye = lax.broadcasted_iota(jnp.int32, (128, 128), 0) == lax.broadcasted_iota(jnp.int32, (128, 128), 1)
    lab_row = jnp.sum(jnp.where(eye, lab_col, 0.0), axis=0, keepdims=True)
    lane = lax.broadcasted_iota(jnp.int32, (1, plan.lanes), 1)
    lane_in = jnp.bitwise_and(lane, BLOCK - 1)
    lane_step = jnp.zeros_like(lane)
    for k in range(1, BLOCK // cap + 1):
        lane_step = lane_step + (lane_in >= k * cap).astype(jnp.int32)
    lane_slot = lane_in - lane_step * cap

    picked, metas = [], []
    for band in range(levels):
        id_col = jnp.full((tile_rows, 1), -1, jnp.int32)
        id_row = jnp.full((1, plan.lanes), -1, jnp.int32)
        for s in range(cap):
            number = ids[0, band, 0, 0, s]
            id_col = jnp.where(slot_of == s, number, id_col)
            id_row = jnp.where(lane_slot == s, number, id_row)
        id_col = jnp.where(used, id_col, -1)
        same_col = (lax.broadcasted_iota(jnp.int32, (tile_rows, cols), 1) == col_of) & used
        total = jnp.zeros((tile_rows, patches.shape[-1]), F32)
        for i in range(rows):
            chosen = jnp.where(same_col & (id_col == i), 1.0, 0.0).astype(BF16)
            total = total + mm(chosen, patches[0, band, i])
        picked.append(total)
        pad = jnp.zeros((1, width - plan.lanes - 128), F32)
        metas.append(jnp.concatenate([id_row.astype(F32), lab_row, pad], axis=1))
    stacked = jnp.concatenate(picked, axis=0).astype(BF16)
    load.wait()
    embedded = mm(stacked, wbuf[...]) + level_embed[...]
    for band in range(levels):
        part = embedded[band * tile_rows : (band + 1) * tile_rows]
        buf[band] = jnp.where(in_block == BLOCK - 1, metas[band], part).astype(BF16)
    pl.semaphore_wait(barrier, len(moves))
    copies = []
    for k, (dm, da, do) in enumerate(moves):
        if do == 0:
            source, target, count = 0, plan.tiles[da][0], tile_rows
        elif do == 1:
            source, target, count = tile_rows - BLOCK, plan.tiles[2 + da][0], BLOCK
        else:
            source, target, count = 0, plan.tiles[4 + da][0], BLOCK
        copies.append(
            pltpu.make_async_remote_copy(
                src_ref=buf.at[band_of[dm], pl.ds(source, count)],
                dst_ref=out.at[me_l, pl.ds(target, count)],
                send_sem=send.at[k],
                recv_sem=recv.at[k],
                device_id=(band_of[dm], lats[da], lons[do]),
                device_id_type=MESH,
            )
        )
    for copy in copies[::-1]:
        copy.start()
    own = pltpu.make_async_copy(buf.at[me_l], out.at[me_l, pl.ds(0, tile_rows)], local)
    own.start()
    own.wait()
    for copy in copies:
        copy.wait()


def main_kernel(
    plan, names, sizes, wide, info, row_code, win, hm, lq, cross_gain, swin_gain, mlp_gain,
    cross_kv, cross_query, cross_out, swin_qkv, swin_out, mlp_up, mlp_down,
    out,
    b_kv, b_query, b_out, b_qkv, b_so, b_up, b_down, start, sems,
):
    levels, _, lon_count = sizes
    pairs = [
        (cross_query, b_query), (cross_kv, b_kv), (cross_out, b_out), (swin_qkv, b_qkv),
        (swin_out, b_so), (mlp_up, b_up), (mlp_down, b_down),
    ]
    loads = [pltpu.make_async_copy(a, b, sems.at[k]) for k, (a, b) in enumerate(pairs)]
    for load in loads:
        load.start()
    l_query, l_kv, l_out, l_qkv, l_so, l_up, l_down = loads
    me_l, me_o = lax.axis_index(names[0]), lax.axis_index(names[2])
    width = lq.shape[1]
    head_dim = width // HEADS
    inv_root = 1.0 / math.sqrt(head_dim)
    latents = lq.shape[0]
    own, count = plan.own, plan.count
    lanes = plan.lanes
    code_c = info[:, 0:1]
    pos_c = info[:, 1:2]
    tile_c = info[:, 2:3]
    lane = lax.broadcasted_iota(jnp.int32, (1, lanes), 1)
    meta_rows = [first + BLOCK - 1 for first, _ in plan.tiles]

    lq_f = lq[...].astype(F32)
    l_query.wait()
    cq = (mm(lq[...], b_query[...]) * inv_root).astype(BF16).astype(F32)
    hm_f = hm[...].astype(F32)
    masked = jnp.concatenate([cq[q : q + 1] * hm_f for q in range(latents)], axis=0).astype(BF16)

    l_kv.wait()
    keys, values, presence = [], [], []
    for level in range(levels):
        tokens = wide[level].astype(F32)
        keys_in = layer_norm(tokens, cross_gain[...]).astype(BF16)
        pair = mm(keys_in, b_kv[...]).astype(BF16)
        id_row = tokens[meta_rows[0] : meta_rows[0] + 1, :lanes]
        for t in range(1, 6):
            first, _ = plan.tiles[t]
            id_row = jnp.where(lane >= first, tokens[meta_rows[t] : meta_rows[t] + 1, :lanes], id_row)
        code_r = (row_code[0:1, :] + id_row.astype(jnp.int32))[:, : plan.wide_rows]
        scatter = jnp.where(
            (code_c == code_r) & (id_row.astype(jnp.int32)[:, : plan.wide_rows] >= 0), 1.0, 0.0
        )
        presence.append(jnp.sum(scatter, axis=1, keepdims=True))
        spread = mm(scatter.astype(BF16), pair)
        keys.append(spread[:, :width].astype(BF16))
        values.append(spread[:, width:])
    lab_src = wide[me_l].astype(F32)
    seg = jnp.zeros((count, 128), F32)
    for t in range(6):
        seg = jnp.where(tile_c == t, lab_src[meta_rows[t] : meta_rows[t] + 1, lanes : lanes + 128], seg)
    at_pos = lax.broadcasted_iota(jnp.int32, (count, 128), 1) == pos_c
    lab_col = jnp.sum(jnp.where(at_pos, seg, 0.0), axis=1, keepdims=True)
    eye = lax.broadcasted_iota(jnp.int32, (count, count), 0) == lax.broadcasted_iota(
        jnp.int32, (count, count), 1
    )
    lab_row = jnp.sum(jnp.where(eye, lab_col, 0.0), axis=0, keepdims=True)
    cell_lane = lax.broadcasted_iota(jnp.int32, (1, count), 1)
    halo = (count - 2 * own) // 2
    bad = ((cell_lane >= 2 * own) & (cell_lane < 2 * own + halo) & (me_o == 0)) | (
        (cell_lane >= 2 * own + halo) & (me_o == lon_count - 1)
    )
    lab_row = jnp.where(bad, -1.0, lab_row)
    allowed = jnp.where(lab_col[:own] == lab_row, win[...], 0.0)
    group = 128 // head_dim
    allowed = jnp.concatenate([allowed] * group, axis=0) > 0.5

    exps = [jnp.exp(mm_nt(keys[l], masked)) * presence[l] for l in range(levels)]
    norm = exps[0]
    for e in exps[1:]:
        norm = norm + e
    weights = [(e / norm).astype(BF16) for e in exps]
    hm_all = jnp.concatenate([hm_f] * latents, axis=0)
    hm_row = lax.broadcasted_iota(jnp.int32, hm_all.shape, 0)
    l_out.wait()
    l_qkv.wait()
    queries, wkeys, wvalues = [], [], []
    for q in range(latents):
        expand = jnp.where(
            (hm_row >= q * HEADS) & (hm_row < (q + 1) * HEADS), hm_all, 0.0
        ).astype(BF16)
        mix = mm(weights[0], expand) * values[0]
        for l in range(1, levels):
            mix = mix + mm(weights[l], expand) * values[l]
        latent = mm(mix.astype(BF16), b_out[...]) + lq_f[q : q + 1]
        start[q * own : (q + 1) * own] = latent[:own]
        normed_f = layer_norm(latent, swin_gain[...])
        normed = normed_f.astype(BF16)
        kv = mm(normed, b_qkv[:, width:]).astype(BF16)
        wkeys.append(kv[:, :width])
        wvalues.append(kv[:, width:])
        queries.append(normed_f[:own])
    q_all = mm(jnp.concatenate(queries, axis=0).astype(BF16), b_qkv[:, :width]) * inv_root
    lane_head = [
        (lax.broadcasted_iota(jnp.int32, (1, 128), 1) >= h * head_dim)
        & (lax.broadcasted_iota(jnp.int32, (1, 128), 1) < (h + 1) * head_dim)
        for h in range(group)
    ]
    mixes = []
    for p in range(latents):
        partners = [k for k in range(latents) if (k + 1) // 2 == (p + 1) // 2]
        pieces = []
        for g in range(width // 128):
            cut = slice(g * 128, (g + 1) * 128)
            part = q_all[p * own : (p + 1) * own, cut]
            stack = jnp.concatenate([jnp.where(h, part, 0.0) for h in lane_head], axis=0).astype(BF16)
            raised = [
                jnp.where(allowed, jnp.exp(mm_nt(stack, wkeys[k][:, cut])), 0.0) for k in partners
            ]
            norm = jnp.sum(raised[0], axis=1, keepdims=True)
            for e in raised[1:]:
                norm = norm + jnp.sum(e, axis=1, keepdims=True)
            inverse = 1.0 / norm
            total = mm((raised[0] * inverse).astype(BF16), wvalues[partners[0]][:, cut])
            for e, k in zip(raised[1:], partners[1:]):
                total = total + mm((e * inverse).astype(BF16), wvalues[k][:, cut])
            piece = jnp.zeros((own, 128), F32)
            for h in range(group):
                piece = jnp.where(lane_head[h], total[h * own : (h + 1) * own], piece)
            pieces.append(piece)
        mixes.append(jnp.concatenate(pieces, axis=1))
    l_so.wait()
    attended = start[...] + mm(jnp.concatenate(mixes, axis=0).astype(BF16), b_so[...])
    mlp_in = layer_norm(attended, mlp_gain[...]).astype(BF16)
    l_up.wait()
    l_down.wait()
    hidden = mlp_up.shape[1]
    result = attended
    step = 512
    for c in range(0, hidden, step):
        up = mm(mlp_in, b_up[:, c : c + step])
        act = (up * (1.0 + lax.erf(up * math.sqrt(0.5))) * 0.5).astype(BF16)
        result = result + mm(act, b_down[c : c + step, :])
    rows, cols = plan.rows, plan.cols
    for p in range(latents):
        for i in range(rows):
            first = (p * rows + i) * cols
            out[p, i] = result[first : first + cols]


def shards(
    sizes, names,
    patches, level_embed, embed_weight, block_ids, latent_queries, cross_gain, cross_query, cross_kv,
    cross_out, region_ids, swin_gain, swin_qkv, swin_out, mlp_gain, mlp_up, mlp_down,
):
    levels = sizes[0]
    _, bands, rows, cols, _ = patches.shape
    width = embed_weight.shape[1]
    plan = Plan(rows, cols, block_ids.shape[-1])
    vmem = pl.BlockSpec(memory_space=pltpu.VMEM)
    hbm = pl.BlockSpec(memory_space=pl.ANY)
    moves = 6 * levels - 1
    wide = pl.pallas_call(
        functools.partial(send_kernel, plan, names, sizes),
        out_shape=jax.ShapeDtypeStruct((levels, plan.wide_rows, width), BF16),
        in_specs=[vmem, vmem, hbm, pl.BlockSpec(memory_space=pltpu.SMEM), vmem],
        out_specs=vmem,
        scratch_shapes=[
            pltpu.VMEM(embed_weight.shape, BF16),
            pltpu.VMEM((bands, plan.tile_rows, width), BF16),
            pltpu.SemaphoreType.DMA,
            pltpu.SemaphoreType.DMA((moves,)),
            pltpu.SemaphoreType.DMA((moves,)),
            pltpu.SemaphoreType.DMA,
        ],
        compiler_params=pltpu.CompilerParams(collective_id=0, has_side_effects=True),
        name="send",
    )(patches, level_embed, embed_weight, block_ids, region_ids)
    latents = latent_queries.shape[0]
    head_mask = (np.arange(width)[None, :] // (width // HEADS) == np.arange(HEADS)[:, None])
    weights = (cross_kv, cross_query, cross_out, swin_qkv, swin_out, mlp_up, mlp_down)
    return pl.pallas_call(
        functools.partial(main_kernel, plan, names, sizes),
        out_shape=jax.ShapeDtypeStruct((latents, rows, cols, width), F32),
        in_specs=[vmem] * 9 + [hbm] * 7,
        out_specs=vmem,
        scratch_shapes=[pltpu.VMEM(w.shape, BF16) for w in weights]
        + [pltpu.VMEM((latents * plan.own, width), F32), pltpu.SemaphoreType.DMA((7,))],
        compiler_params=pltpu.CompilerParams(vmem_limit_bytes=56 << 20),
        name="main",
    )(
        wide, jnp.asarray(plan.info), jnp.asarray(plan.row_code), jnp.asarray(plan.win),
        jnp.asarray(head_mask, BF16), latent_queries, cross_gain.reshape(1, -1),
        swin_gain.reshape(1, -1), mlp_gain.reshape(1, -1), *weights,
    )


def solution(mesh):
    names = ("lvl", "lat", "lon")
    sizes = tuple(mesh.shape[name] for name in names)
    tiled = P("lvl", None, "lat", "lon", None)
    return jax.shard_map(
        functools.partial(shards, sizes, names),
        mesh=mesh,
        in_specs=(
            tiled, P("lvl", None), P(), tiled, P(), P(), P(), P(), P(), P(("lvl", "lat"), "lon"),
            P(), P(), P(), P(), P(), P(),
        ),
        out_specs=P(None, ("lvl", "lat"), "lon", None),
        check_vma=False,
    )
```
